32 devices in a mesh: groups: 2 (over y), lists: 8 (over z, x), rep: 2 (over core).
Axes of the slice: x: 2, y: 2, z: 4, core: 2. Of those that a mesh axis runs over, the one named last changes fastest.
Arguments:
- queries: bfloat16 [512, 1024], P(('groups', 'lists', 'rep')), parts along dimension 0
- corpus: bfloat16 [64, 1024, 1024], P(('groups', 'lists')), parts along dimension 0
- list_slot: int32 [64], P('groups'), parts along dimension 0, may hold values from 0 to 31, each once
- probes: int32 [512, 8], P(('groups', 'lists', 'rep')), parts along dimension 0, may hold values from 0 to 31, all different within a row; in each aligned block of 16 rows (0 to 15, 16 to 31, ...) at most 8 rows name the same one
- cand: int32 [512, 8, 2], P(('groups', 'lists', 'rep')), parts along dimension 0, may hold values from 0 to 7
Outputs:
- scores: bfloat16 [512, 8, 2, 128], P(('groups', 'lists', 'rep')), parts along dimension 0
The draws below stay inside these ranges and needn't reach their ends.
There are 2 independent parts, one for each index of `groups`. The reference program is written for one: setup_inputs(seed, part) draws one part's arguments, and reference() takes and returns one part's arrays. A program takes and returns all parts, laid end to end along the dimension named above; each array names one. Nothing has to cross between parts.
Inputs may be any that keep to these rules, and one draw needn't show every extreme that they name: A permutation: list L is stored at position list_slot[L] of corpus. `probes`: each row names 8 different lists; in the 16 rows of one device no list is named by more than 8 rows, and in some device's rows one list is named by exactly 8. `cand`: index of a block of 128 consecutive rows within the probed list.
All inputs are finite; a program needn't handle non-finite values.
Results may differ from the reference program's by a relative error of at most 0.001.
Values may be sent and summed in bfloat16 or wider, within the bound.
A program may use at most 64 MiB of HBM per device.

```python
import math
import jax
import jax.numpy as jnp
import numpy as np
from jax import lax

D = 1024
LIST_ROWS = 1024
Q_DEV = 16
PROBES = 8
CAND = 2
BLOCK = 128
LISTS = 32
QUERIES = 256
MOST = 8
NBLK = 8
N_LISTS = 8
N_REP = 2


def scaled_normal(key, array_shape):
    key_base = jax.random.fold_in(key, 11)
    key_rows = jax.random.fold_in(key, 23)
    key_cols = jax.random.fold_in(key, 37)
    row_scale = jnp.exp(jax.random.uniform(key_rows, array_shape[:-1] + (1,), jnp.float32) * math.log(10.0))
    col_scale = jnp.exp(jax.random.uniform(key_cols, (array_shape[-1],), jnp.float32) * math.log(10.0))
    entries = jax.random.normal(key_base, array_shape, jnp.float32)
    return (entries * row_scale * col_scale).astype(jnp.bfloat16)


def draw_queries(key, part):
    return scaled_normal(jax.random.fold_in(key, 101), (QUERIES, D))


def draw_corpus(key, part):
    return scaled_normal(jax.random.fold_in(key, 202), (LISTS, LIST_ROWS, D))


def set_ends(values, rng, least, top_value):
    place = [jax.random.randint(jax.random.fold_in(rng, axis), (), 0, length) for axis, length in enumerate(values.shape)]
    main_axis = values.shape.index(max(values.shape))
    neighbour = place[:main_axis] + [(place[main_axis] + 1) % values.shape[main_axis]] + place[main_axis + 1:]
    return values.at[tuple(place)].set(least).at[tuple(neighbour)].set(top_value)


def assign_block(key, own, number, rows, amount, top, reach, slope):
    sequence = jax.random.permutation(key, amount)
    packed, usual = shares(amount, rows * top, reach, slope, True), shares(amount, rows * top, reach, slope, False)
    places = jnp.arange(amount)

    def named(lengths, rotation):
        used = int((lengths > 0).sum())
        fixed = max(1, used // 4)
        passed = fixed + (places - fixed + rotation * (used - fixed)) % max(1, amount - fixed)
        return jnp.zeros((amount,), jnp.int32).at[sequence[jnp.where(places < fixed, places, passed)]].set(jnp.asarray(lengths, jnp.int32))

    lengths = jnp.where(number % 4 == 0, named(packed, number // 4), named(usual, number - number // 4 - 1))
    mixed = jax.random.permutation(jax.random.fold_in(own, 3), amount)
    source_of, receiver = mixed[0:amount // 2 * 2:2], mixed[1:amount // 2 * 2:2]
    room = jnp.minimum(lengths[source_of] - 1, reach - lengths[receiver]) // 2
    room = jnp.where((source_of == sequence[0]) | (receiver == sequence[0]) | (lengths[receiver] == 0), 0, jnp.maximum(room, 0))
    passed = jax.random.randint(jax.random.fold_in(own, 4), (amount // 2,), 0, 1 << 20) % (room + 1)
    lengths = lengths.at[source_of].add(-passed).at[receiver].add(passed)
    members = jnp.searchsorted(jnp.cumsum(lengths), jnp.arange(rows * top), side="right").astype(jnp.int32)
    grid = members.reshape(top, rows).T
    grid = grid[jax.random.permutation(jax.random.fold_in(own, 1), rows)]
    rotation = jax.random.randint(jax.random.fold_in(own, 2), (rows, 1), 0, top)
    return jnp.take_along_axis(grid, (jnp.arange(top)[None, :] + rotation) % top, axis=1)


def shares(number_of, total, reach, skew, full):
    weights = [(1 << 20) // math.isqrt(rank ** skew) + 1 for rank in range(1, number_of + 1)]
    largest = reach if full else min(reach, max(-(-total // number_of), total * weights[0] // sum(weights)))
    least = 1 if total - largest >= number_of - 1 else 0
    holding, spare = [largest] + [least] * (number_of - 1), total - largest - least * (number_of - 1)
    while spare > 0:
        movable = [i for i in range(1, number_of) if holding[i] < largest] or [i for i in range(1, number_of) if holding[i] < reach]
        mass, left = sum([weights[i] for i in movable]), spare
        for i in movable:
            extra = min(reach - holding[i], max(1, left * weights[i] // mass), spare)
            holding[i] = holding[i] + extra
            spare = spare - extra
    return np.array(holding)


def setup_inputs(seed: int = 0, part: int = 0) -> dict:
    key_list = jax.random.split(jax.random.key(seed), 6)
    part_splits = jax.random.split(jax.random.fold_in(key_list[5], part), 6)
    queries = draw_queries(jax.random.fold_in(jax.random.fold_in(key_list[5], part), 71), part)
    corpus = draw_corpus(jax.random.fold_in(jax.random.fold_in(key_list[5], part), 71), part)
    list_slot = jax.random.permutation(part_splits[2], LISTS).astype(jnp.int32)
    probes_keys = jax.random.split(jax.random.fold_in(part_splits[3], 1), QUERIES // Q_DEV)
    probes_turns = jax.random.permutation(jax.random.fold_in(part_splits[3], 3), QUERIES // Q_DEV)
    probes = jax.vmap(lambda own, number: assign_block(jax.random.fold_in(part_splits[3], 2), own, number, Q_DEV, LISTS, PROBES, MOST, 2))(probes_keys, probes_turns).reshape((QUERIES, PROBES))
    cand = set_ends(jax.random.randint(part_splits[4], (QUERIES, PROBES, CAND), 0, NBLK), jax.random.fold_in(part_splits[4], 1), 0, NBLK - 1).astype(jnp.int32)
    return dict(queries=queries, corpus=corpus, list_slot=list_slot, probes=probes, cand=cand)


epsilon = 1e-06

def inverse_norm(values):
    squares = jnp.einsum('...d,...d->...', values, values, preferred_element_type=jnp.float32)
    return lax.rsqrt(squares / values.shape[-1] + epsilon)

def reference(queries, corpus, list_slot, probes, cand):
    pair_count = QUERIES * PROBES
    list_room = N_LISTS * N_REP * MOST
    inv_rows = inverse_norm(corpus)
    inv_queries = inverse_norm(queries)
    pair_slot = list_slot[probes.reshape(pair_count)].astype(jnp.int32)
    pair_query = jnp.arange(pair_count, dtype=jnp.int32) // PROBES
    pair_cand = cand.reshape(pair_count, CAND).astype(jnp.int32)

    def one_list(totals, slot_id):
        pair_order = jnp.argsort((pair_slot != slot_id).astype(jnp.int32), stable=True)[:list_room].astype(jnp.int32)
        chosen = pair_slot[pair_order] == slot_id
        owners = pair_query[pair_order]
        vectors = queries[owners]
        listed = lax.dynamic_index_in_dim(corpus, slot_id, 0, keepdims=False)
        list_inv = lax.dynamic_index_in_dim(inv_rows, slot_id, 0, keepdims=False)
        products = jnp.dot(vectors, listed.T, preferred_element_type=jnp.float32)
        scaled = products * inv_queries[owners][:, None] * list_inv[None, :] * D ** (-0.5)
        blocks = scaled.astype(jnp.bfloat16).reshape(list_room, NBLK, BLOCK)
        selected = blocks[jnp.arange(list_room, dtype=jnp.int32)[:, None], pair_cand[pair_order]]
        target = jnp.where(chosen, pair_order, pair_count)
        totals = totals.at[target].set(selected, mode='drop')
        return (totals, None)
    blank_scores = jnp.zeros((pair_count, CAND, BLOCK), jnp.bfloat16)
    result, _ = lax.scan(one_list, blank_scores, jnp.arange(LISTS, dtype=jnp.int32))
    return result.reshape(QUERIES, PROBES, CAND, BLOCK)
```

```python
import functools

import jax
import jax.numpy as jnp
from jax import lax
from jax.experimental import pallas as pl
from jax.experimental.pallas import tpu as pltpu
from jax.sharding import PartitionSpec as P

BLOCK = 128
LANES = 128
epsilon = 1e-06
f32, bf16 = jnp.float32, jnp.bfloat16
NN = (((1,), (0,)), ((), ()))
NT = (((1,), (1,)), ((), ()))


def dot(a, b, dims=NN):
    return lax.dot_general(a, b, dims, preferred_element_type=f32)


def iota(shape, axis):
    return lax.broadcasted_iota(jnp.int32, shape, axis)


def repeat(start, stop, body):
    if stop - start <= 8:
        for i in range(start, stop):
            body(i)
    else:
        lax.fori_loop(start, stop, lambda i, c: (body(i), c)[1], 0)


def kernel(
    owners, queries, corpus, list_slot, probes, cand, out,
    all_q, lists, table, all_table, place, gathered, choice, inv_q, inv_rows, picked, reply, replies,
    q_send, q_recv, t_send, t_recv, r_send, r_recv, list_sem,
):
    me = lax.axis_index("lists")
    local, length, features = lists.shape
    count = all_q.shape[1]
    total = list_slot.shape[1]
    probe_count = probes.shape[0]
    cand_count = cand.shape[1]
    room = table.shape[1] // local
    slots = table.shape[1]

    def peer(i):
        return lax.rem(me + i, owners)

    def remote(src, dst, send, recv, i):
        return pltpu.make_async_remote_copy(
            src_ref=src, dst_ref=dst, send_sem=send.at[i], recv_sem=recv.at[me],
            device_id={"lists": peer(i)}, device_id_type=pl.DeviceIdType.MESH,
        )

    def arrived(dst, recv, who):
        pltpu.make_async_copy(dst, dst, recv.at[who]).wait()

    barrier = pltpu.get_barrier_semaphore()
    repeat(1, owners, lambda i: pl.semaphore_signal(
        barrier, inc=1, device_id={"lists": peer(i)}, device_id_type=pl.DeviceIdType.MESH))

    own_q = pltpu.make_async_copy(queries, all_q.at[me], q_recv.at[me])
    own_q.start()
    for l in range(local):
        pltpu.make_async_copy(corpus.at[l], lists.at[l], list_sem.at[l]).start()

    ids = iota((total, count), 0)
    named = jnp.zeros((total, count), f32)
    turn = jnp.zeros((total, count), f32)
    wanted = [jnp.zeros((total, count), f32) for _ in range(cand_count)]
    for p in range(probe_count):
        hit = ids == probes[p : p + 1, :]
        named = jnp.where(hit, 1.0, named)
        turn = jnp.where(hit, float(p), turn)
        for c in range(cand_count):
            wanted[c] = jnp.where(hit, cand[p, c : c + 1, :].astype(f32), wanted[c])
    turn = turn + named * (iota((total, count), 1) * probe_count + 1).astype(f32)
    to_slot = (iota((total, total), 0) == list_slot[...]).astype(bf16)
    here = dot(to_slot, named.astype(bf16)).astype(bf16)
    kinds = [here] + [dot(to_slot, w.astype(bf16)).astype(bf16) for w in wanted + [turn]]
    lane = iota((count, LANES), 1)
    row = iota((count, LANES), 0)
    spread = ((lane % count) == row) & (lane < count * len(kinds))
    value = sum(dot(k, (lane == row + i * count).astype(bf16)) for i, k in enumerate(kinds))
    taken = dot(here, spread.astype(bf16))
    rank = dot(here, (row < lane % count).astype(bf16))
    rank = jnp.where(taken > 0.5, rank, -1.0)
    rank = lax.broadcast_in_dim(rank, (total, room, LANES), (0, 2))
    value = lax.broadcast_in_dim(value, (total, room, LANES), (0, 2))
    entry = jnp.where(rank == iota((total, room, LANES), 1).astype(f32), value, 0.0)
    table[...] = entry.astype(bf16).reshape(table.shape)

    pl.semaphore_wait(barrier, owners - 1)
    repeat(1, owners, lambda i: remote(queries, all_q.at[me], q_send, q_recv, i).start())
    repeat(1, owners, lambda i: remote(table.at[peer(i)], all_table.at[me], t_send, t_recv, i).start())
    own_t = pltpu.make_async_copy(table.at[me], all_table.at[me], t_recv.at[me])
    own_t.start()

    kind = iota((8, LANES), 1)
    last = count * (cand_count + 1)
    pick_turn = ((kind >= last) & (kind < last + count)).astype(bf16)
    target = dot(pick_turn, entry.astype(bf16).reshape(total * room, LANES), NT)[:1].astype(jnp.int32) - 1
    out_rows = iota((out.shape[0], total * room), 0)
    for c in range(cand_count):
        place[c] = (out_rows == target * cand_count + c).astype(bf16)

    step = min(length, 256)
    ones = jnp.ones((8, LANES), bf16)
    for l in range(local):
        pltpu.make_async_copy(corpus.at[l], lists.at[l], list_sem.at[l]).wait()

        def norms(k, carry):
            at = pl.multiple_of(k * step, step)
            part = jnp.zeros((step, LANES), f32)
            for j in range(0, features, LANES):
                x = lists[l, pl.ds(at, step), j : j + LANES].astype(f32)
                part = part + x * x
            high = part.astype(bf16)
            rest = part - high.astype(f32)
            mid = rest.astype(bf16)
            low = (rest - mid.astype(f32)).astype(bf16)
            squares = dot(ones, high, NT) + (dot(ones, mid, NT) + dot(ones, low, NT))
            inv_rows[l, :, pl.ds(at, step)] = lax.rsqrt(squares / features + epsilon)
            return carry

        lax.fori_loop(0, length // step, norms, 0)

    kind_row = iota((LANES, cand_count * LANES), 0)
    kind_lane = iota((LANES, cand_count * LANES), 1) // LANES
    pick_cand = (kind_row // count == kind_lane + 1).astype(bf16)

    def gather(i):
        who = peer(owners - i)
        arrived(all_q.at[who], q_recv, who)
        arrived(all_table.at[who], t_recv, who)
        info = all_table[who]
        rows = dot(info[:, :count], all_q[who])
        chosen = dot(info, pick_cand)
        inverse = lax.rsqrt(jnp.sum(rows * rows, axis=1, keepdims=True) / features + epsilon)
        inverse = jnp.broadcast_to(inverse, (slots, LANES))
        at = pl.ds(pl.multiple_of(who * room, room), room)
        for l in range(local):
            mine = slice(l * room, (l + 1) * room)
            gathered[l, at, :] = rows[mine]
            choice[l, at, :] = chosen[mine]
            inv_q[l, at, :] = inverse[mine]

    repeat(0, owners, gather)

    scale = features ** (-0.5)

    def score(l, carry):
        products = dot(gathered[l].astype(bf16), lists[l], NT)
        inverse = inv_q[l]
        blocks = []
        for b in range(length // BLOCK):
            inv_b = inv_rows[l, :1, b * BLOCK : (b + 1) * BLOCK]
            blocks.append(products[:, b * BLOCK : (b + 1) * BLOCK] * inverse * inv_b * scale)
        for c in range(cand_count):
            want = choice[l, :, c * LANES : (c + 1) * LANES]
            best = blocks[0]
            for b in range(1, length // BLOCK):
                best = jnp.where(want == float(b), blocks[b], best)
            picked[:, pl.ds(pl.multiple_of(l * room, room), room), c * LANES : (c + 1) * LANES] = best.reshape(
                owners, room, LANES)
        return carry

    lax.fori_loop(0, local, score, 0)
    reply[...] = picked[...].astype(bf16)
    own_r = pltpu.make_async_copy(reply.at[me], replies.at[me], r_recv.at[me])
    own_r.start()
    repeat(1, owners, lambda i: remote(reply.at[peer(i)], replies.at[me], r_send, r_recv, i).start())
    repeat(0, owners, lambda i: arrived(replies.at[peer(owners - i)], r_recv, peer(owners - i)))

    result = jnp.zeros(out.shape, f32)
    for c in range(cand_count):
        back = replies[:, :, c * LANES : (c + 1) * LANES].reshape(total * room, LANES)
        result = result + dot(place[c], back)
    out[...] = result.astype(bf16)

    def sent(i):
        remote(queries, all_q.at[me], q_send, q_recv, i).wait_send()
        remote(table.at[peer(i)], all_table.at[me], t_send, t_recv, i).wait_send()
        remote(reply.at[peer(i)], replies.at[me], r_send, r_recv, i).wait_send()

    repeat(1, owners, sent)


def on_device(queries, corpus, list_slot, probes, cand):
    owners = lax.axis_size("lists")
    count, features = queries.shape
    probe_count = probes.shape[1]
    cand_count = cand.shape[2]
    local, length, _ = corpus.shape
    total = list_slot.shape[0]
    pairs = count * probe_count
    most = min(count, max(2, (2 * pairs + total - 1) // total))
    room = -(-most // 8) * 8
    slots = local * room
    vmem = pl.BlockSpec(memory_space=pltpu.VMEM)
    hbm = pl.BlockSpec(memory_space=pltpu.HBM)
    out = pl.pallas_call(
        functools.partial(kernel, owners),
        out_shape=jax.ShapeDtypeStruct((pairs * cand_count, BLOCK), bf16),
        in_specs=[hbm, hbm, vmem, vmem, vmem],
        out_specs=vmem,
        scratch_shapes=[
            pltpu.VMEM((owners, count, features), bf16),
            pltpu.VMEM(corpus.shape, bf16),
            pltpu.VMEM((owners, slots, LANES), bf16),
            pltpu.VMEM((owners, slots, LANES), bf16),
            pltpu.VMEM((cand_count, pairs * cand_count, total * room), bf16),
            pltpu.VMEM((local, owners * room, features), f32),
            pltpu.VMEM((local, owners * room, cand_count * LANES), f32),
            pltpu.VMEM((local, owners * room, LANES), f32),
            pltpu.VMEM((local, 8, length), f32),
            pltpu.VMEM((owners, slots, cand_count * LANES), f32),
            pltpu.VMEM((owners, slots, cand_count * LANES), bf16),
            pltpu.VMEM((owners, slots, cand_count * LANES), bf16),
        ] + [pltpu.SemaphoreType.DMA((owners,))] * 6 + [pltpu.SemaphoreType.DMA((local,))],
        compiler_params=pltpu.CompilerParams(collective_id=0, has_side_effects=True, vmem_limit_bytes=48 * 2**20),
    )(queries, corpus, list_slot.reshape(1, total), probes.T, cand.transpose(1, 2, 0))
    return out.reshape(count, probe_count, cand_count, BLOCK)


def solution(mesh):
    placed = (
        P(("groups", "lists", "rep"), None),
        P(("groups", "lists"), None, None),
        P("groups"),
        P(("groups", "lists", "rep"), None),
        P(("groups", "lists", "rep"), None, None),
    )
    return jax.shard_map(
        on_device,
        mesh=mesh,
        in_specs=placed,
        out_specs=P(("groups", "lists", "rep"), None, None, None),
        check_vma=False,
    )
```

```python
import functools

import jax
import jax.numpy as jnp
from jax import lax
from jax.experimental import pallas as pl
from jax.experimental.pallas import tpu as pltpu
from jax.sharding import PartitionSpec as P

BLOCK = 128
LANES = 128
epsilon = 1e-06
f32, bf16 = jnp.float32, jnp.bfloat16
NN = (((1,), (0,)), ((), ()))
NT = (((1,), (1,)), ((), ()))


def dot(a, b, dims=NN):
    return lax.dot_general(a, b, dims, preferred_element_type=f32)


def iota(shape, axis):
    return lax.broadcasted_iota(jnp.int32, shape, axis)


def repeat(start, stop, body):
    if stop - start <= 8:
        for i in range(start, stop):
            body(i)
    else:
        lax.fori_loop(start, stop, lambda i, c: (body(i), c)[1], 0)


def kernel(
    owners, queries, corpus, list_slot, probes, cand, out,
    all_q, lists, slot_of, all_probes, all_cand, place, pick, choice, gathered, inv_q, inv_rows, reply, replies,
    q_send, q_recv, p_send, p_recv, c_send, c_recv, r_send, r_recv, list_sem, slot_sem,
):
    me = lax.axis_index("lists")
    local, length, features = lists.shape
    count = all_q.shape[1]
    total = list_slot.shape[1]
    probe_count = probes.shape[0]
    cand_count = cand.shape[1]
    room = replies.shape[2]
    pairs_of = owners // 2
    mate = me + 1 - 2 * (me % 2)
    side, spot = me % 2, me // 2

    def far(t):
        down = pairs_of - 1 - t
        down = down - jnp.where(down <= spot, 1, 0)
        up = t + jnp.where(t >= spot, 1, 0)
        return jnp.where(spot < pairs_of // 2, down, up)

    def other(i):
        if isinstance(i, int) and i == owners - 2:
            return mate
        there = 2 * far(i // 2) + i % 2
        return there if isinstance(i, int) else jnp.where(i == owners - 2, mate, there)

    def remote(src, dst, send, recv, who):
        return pltpu.make_async_remote_copy(
            src_ref=src, dst_ref=dst, send_sem=send, recv_sem=recv,
            device_id={"lists": who}, device_id_type=pl.DeviceIdType.MESH,
        )

    def arrived(dst, sem):
        pltpu.make_async_copy(dst, dst, sem).wait()

    def send_meta(i):
        who = other(i)
        return (remote(probes, all_probes.at[me], p_send.at[i], p_recv.at[me], who),
                remote(cand, all_cand.at[me], c_send.at[i], c_recv.at[me], who))

    def send_query(t):
        return remote(queries, all_q.at[me], q_send.at[t], q_recv.at[me], 2 * far(t) + side)

    def send_mate():
        return remote(queries, all_q.at[me], q_send.at[pairs_of - 1], q_recv.at[me], mate)

    def relay(t):
        who = 2 * far(pairs_of - 2 - t) + side
        return who, remote(all_q.at[who], all_q.at[who], q_send.at[pairs_of + t], q_recv.at[who], mate)

    def send_reply(l, i):
        who = other(i)
        return remote(reply.at[l, who], replies.at[l, me], r_send.at[l, i], r_recv.at[l, me], who)

    barrier = pltpu.get_barrier_semaphore()
    repeat(0, owners - 1, lambda i: pl.semaphore_signal(
        barrier, inc=1, device_id={"lists": other(i)}, device_id_type=pl.DeviceIdType.MESH))

    get_slot = pltpu.make_async_copy(list_slot, slot_of, slot_sem)
    get_slot.start()
    pltpu.make_async_copy(probes, all_probes.at[me], p_recv.at[me]).start()
    pltpu.make_async_copy(cand, all_cand.at[me], c_recv.at[me]).start()
    pltpu.make_async_copy(queries, all_q.at[me], q_recv.at[me]).start()
    for l in range(local):
        pltpu.make_async_copy(corpus.at[l], lists.at[l], list_sem.at[l]).start()

    pl.semaphore_wait(barrier, owners - 1)
    repeat(0, owners - 1, lambda i: [c.start() for c in send_meta(i)])
    send_mate().start()
    repeat(0, pairs_of - 1, lambda t: send_query(t).start())

    get_slot.wait()
    arrived(all_probes.at[me], p_recv.at[me])
    mine = all_probes[me]
    ids = iota((total, count), 0)
    named = jnp.zeros((total, count), f32)
    turn = jnp.zeros((total, count), f32)
    for p in range(probe_count):
        hit = ids == mine[p : p + 1, :]
        named = jnp.where(hit, 1.0, named)
        turn = jnp.where(hit, float(p), turn)
    turn = turn + named * (iota((total, count), 1) * probe_count + 1).astype(f32)
    held = iota((total, total), 0)
    to_slot = ((held % owners) * local + held // owners == slot_of[...]).astype(bf16)
    here = dot(to_slot, named.astype(bf16)).astype(bf16)
    turn = dot(to_slot, turn.astype(bf16))
    rank = dot(here, (iota((count, count), 0) < iota((count, count), 1)).astype(bf16))
    rank = lax.broadcast_in_dim(rank, (total, room, count), (0, 2))
    turn = lax.broadcast_in_dim(turn, (total, room, count), (0, 2))
    entry = jnp.where(rank == iota((total, room, count), 1).astype(f32), turn, 0.0)
    entry = entry.reshape(total * room, count).astype(bf16)
    target = dot(jnp.ones((8, count), bf16), entry, NT)[:1].astype(jnp.int32) - 1
    out_rows = iota((out.shape[0], total * room), 0)
    for c in range(cand_count):
        place[c] = (out_rows == target * cand_count + c).astype(bf16)

    step = min(length, 256)
    ones = jnp.ones((8, LANES), bf16)

    def norms_of(l):
        pltpu.make_async_copy(corpus.at[l], lists.at[l], list_sem.at[l]).wait()

        def norms(k, carry):
            at = pl.multiple_of(k * step, step)
            part = jnp.zeros((step, LANES), f32)
            for j in range(0, features, LANES):
                x = lists[l, pl.ds(at, step), j : j + LANES].astype(f32)
                part = part + x * x
            high = part.astype(bf16)
            rest = part - high.astype(f32)
            mid = rest.astype(bf16)
            low = (rest - mid.astype(f32)).astype(bf16)
            squares = dot(ones, high, NT) + (dot(ones, mid, NT) + dot(ones, low, NT))
            inv_rows[l, :, pl.ds(at, step)] = lax.rsqrt(squares / features + epsilon)
            return carry

        lax.fori_loop(0, length // step, norms, 0)

    def forward(t):
        who, copy = relay(t)
        arrived(all_q.at[who], q_recv.at[who])
        copy.start()

    norms_of(0)
    forward(0) if pairs_of > 1 else None
    for l in range(1, local):
        norms_of(l)
        if l < pairs_of - 1:
            forward(l)
    repeat(min(max(local, 1), pairs_of - 1), pairs_of - 1, forward)

    some = LANES // count
    rows = some * room
    lane = iota((rows, LANES), 1)
    row = iota((rows, LANES), 0)
    same = row // room == lane // count
    before = ((iota((LANES, LANES), 0) < iota((LANES, LANES), 1))
              & (iota((LANES, LANES), 0) // count == iota((LANES, LANES), 1) // count)).astype(bf16)

    def meta_here(o):
        @pl.when(o != me)
        def _():
            arrived(all_probes.at[o], p_recv.at[o])
        arrived(all_cand.at[o], c_recv.at[o])

    repeat(0, owners, meta_here)

    def index(k):
        asked = jnp.concatenate([all_probes[k * some + i] for i in range(some)], axis=1)
        blocks = [jnp.concatenate([all_cand[k * some + i, :, c, :] for i in range(some)], axis=1).astype(f32)
                  for c in range(cand_count)]
        at = pl.ds(k * rows, rows)
        for l in range(local):
            name = jnp.sum(jnp.where(slot_of[...] == me * local + l, iota((1, total), 1), 0), axis=1, keepdims=True)
            hit = asked == name
            named = jnp.sum(jnp.where(hit, 1.0, 0.0), axis=0, keepdims=True)
            rank = dot(jnp.broadcast_to(named, (8, LANES)).astype(bf16), before)[:1]
            rank = jnp.where(named > 0.5, rank, -1.0)
            taken = same & (rank == (row % room).astype(f32))
            pick[l, at, :] = jnp.where(taken, 1.0, 0.0).astype(bf16)
            for c in range(cand_count):
                want = jnp.sum(jnp.where(hit, blocks[c], 0.0), axis=0, keepdims=True)
                want = jnp.where(taken, want, 0.0).astype(bf16)
                choice[l, at, c * LANES : (c + 1) * LANES] = dot(want, jnp.ones((LANES, LANES), bf16))

    repeat(0, owners // some, index)

    arrived(all_q.at[me], q_recv.at[me])
    repeat(0, pairs_of, lambda t: arrived(all_q.at[2 * t + 1 - side], q_recv.at[2 * t + 1 - side]))

    scale = features ** (-0.5)

    def score(l, carry):
        def gather(k):
            at = pl.ds(k * rows, rows)
            chunk = all_q[pl.ds(k * some, some)].reshape(some * count, features)
            got = dot(pick[l, at, :], chunk)
            inverse = lax.rsqrt(jnp.sum(got * got, axis=1, keepdims=True) / features + epsilon)
            inv_q[at, :] = jnp.broadcast_to(inverse, (rows, LANES))
            gathered[at, :] = got.astype(bf16)

        repeat(0, owners // some, gather)
        products = dot(gathered[...], lists[l], NT)
        inverse = inv_q[...]
        blocks = []
        for b in range(length // BLOCK):
            inv_b = inv_rows[l, :1, b * BLOCK : (b + 1) * BLOCK]
            blocks.append(products[:, b * BLOCK : (b + 1) * BLOCK] * inverse * inv_b * scale)
        for c in range(cand_count):
            want = choice[l, :, c * LANES : (c + 1) * LANES]
            best = blocks[0]
            for b in range(1, length // BLOCK):
                best = jnp.where(want == float(b), blocks[b], best)
            reply[l, :, :, c * LANES : (c + 1) * LANES] = best.reshape(owners, room, LANES).astype(bf16)
        repeat(0, owners - 1, lambda i: send_reply(l, i).start())
        pltpu.make_async_copy(reply.at[l, me], replies.at[l, me], r_recv.at[l, me]).start()
        return carry

    lax.fori_loop(0, local, score, 0)

    def answers(l, carry):
        repeat(0, owners, lambda o: arrived(replies.at[l, o], r_recv.at[l, o]))
        return carry

    lax.fori_loop(0, local, answers, 0)

    result = jnp.zeros(out.shape, f32)
    for c in range(cand_count):
        back = replies[:, :, :, c * LANES : (c + 1) * LANES].reshape(total * room, LANES)
        result = result + dot(place[c], back)
    out[...] = result.astype(bf16)

    send_mate().wait_send()
    repeat(0, pairs_of - 1, lambda t: send_query(t).wait_send())
    repeat(0, pairs_of - 1, lambda t: relay(t)[1].wait_send())
    repeat(0, owners - 1, lambda i: [c.wait_send() for c in send_meta(i)])

    def sent(l, carry):
        repeat(0, owners - 1, lambda i: send_reply(l, i).wait_send())
        return carry

    lax.fori_loop(0, local, sent, 0)


def on_device(queries, corpus, list_slot, probes, cand):
    owners = lax.axis_size("lists")
    count, features = queries.shape
    probe_count = probes.shape[1]
    cand_count = cand.shape[2]
    local, length, _ = corpus.shape
    total = list_slot.shape[0]
    pairs = count * probe_count
    most = min(count, max(2, (2 * pairs + total - 1) // total))
    room = -(-most // 8) * 8
    vmem = pl.BlockSpec(memory_space=pltpu.VMEM)
    hbm = pl.BlockSpec(memory_space=pltpu.HBM)
    dma = pltpu.SemaphoreType.DMA
    wide = cand_count * LANES
    out = pl.pallas_call(
        functools.partial(kernel, owners),
        out_shape=jax.ShapeDtypeStruct((pairs * cand_count, BLOCK), bf16),
        in_specs=[hbm] * 5,
        out_specs=vmem,
        scratch_shapes=[
            pltpu.VMEM((owners, count, features), bf16),
            pltpu.VMEM(corpus.shape, bf16),
            pltpu.VMEM((1, total), jnp.int32),
            pltpu.VMEM((owners, probe_count, count), jnp.int32),
            pltpu.VMEM((owners, probe_count, cand_count, count), jnp.int32),
            pltpu.VMEM((cand_count, pairs * cand_count, total * room), bf16),
            pltpu.VMEM((local, owners * room, LANES), bf16),
            pltpu.VMEM((local, owners * room, wide), f32),
            pltpu.VMEM((owners * room, features), bf16),
            pltpu.VMEM((owners * room, LANES), f32),
            pltpu.VMEM((local, 8, length), f32),
            pltpu.VMEM((local, owners, room, wide), bf16),
            pltpu.VMEM((local, owners, room, wide), bf16),
            dma((owners,)), dma((owners,)), dma((owners,)), dma((owners,)), dma((owners,)), dma((owners,)),
            dma((local, owners)), dma((local, owners)), dma((local,)), dma,
        ],
        compiler_params=pltpu.CompilerParams(collective_id=0, has_side_effects=True, vmem_limit_bytes=67043328),
    )(queries, corpus, list_slot.reshape(1, total), probes.T, cand.transpose(1, 2, 0))
    return out.reshape(count, probe_count, cand_count, BLOCK)


def solution(mesh):
    placed = (
        P(("groups", "lists", "rep"), None),
        P(("groups", "lists"), None, None),
        P("groups"),
        P(("groups", "lists", "rep"), None),
        P(("groups", "lists", "rep"), None, None),
    )
    return jax.shard_map(
        on_device,
        mesh=mesh,
        in_specs=placed,
        out_specs=P(("groups", "lists", "rep"), None, None, None),
        check_vma=False,
    )
```

```python
import functools

import jax
import jax.numpy as jnp
from jax import lax
from jax.experimental import pallas as pl
from jax.experimental.pallas import tpu as pltpu
from jax.sharding import PartitionSpec as P

BLOCK = 128
LANES = 128
epsilon = 1e-06
f32, bf16 = jnp.float32, jnp.bfloat16
NN = (((1,), (0,)), ((), ()))
NT = (((1,), (1,)), ((), ()))


def dot(a, b, dims=NN):
    return lax.dot_general(a, b, dims, preferred_element_type=f32)


def iota(shape, axis):
    return lax.broadcasted_iota(jnp.int32, shape, axis)


def repeat(start, stop, body):
    if stop - start <= 8:
        for i in range(start, stop):
            body(i)
    else:
        lax.fori_loop(start, stop, lambda i, c: (body(i), c)[1], 0)


def kernel(
    owners, queries, corpus, list_slot, probes, cand, out,
    all_q, lists, slot_of, own_probes, own_cand, all_meta, place, pick, choice, inv_q, inv_rows, reply, replies,
    q_send, q_recv, m_send, m_recv, r_send, r_recv, list_sem, slot_sem, probe_sem, cand_sem,
):
    me = lax.axis_index("lists")
    local, length, features = lists.shape
    count = all_q.shape[1]
    total = list_slot.shape[1]
    probe_count = probes.shape[0]
    cand_count = cand.shape[1]
    room = replies.shape[2]
    pairs_of = owners // 2
    mate = me + 1 - 2 * (me % 2)
    side, spot = me % 2, me // 2

    def far(t):
        down = pairs_of - 1 - t
        down = down - jnp.where(down <= spot, 1, 0)
        up = t + jnp.where(t >= spot, 1, 0)
        return jnp.where(spot < pairs_of // 2, down, up)

    def other(i):
        if isinstance(i, int) and i == owners - 2:
            return mate
        there = 2 * far(i // 2) + i % 2
        return there if isinstance(i, int) else jnp.where(i == owners - 2, mate, there)

    def remote(src, dst, send, recv, who):
        return pltpu.make_async_remote_copy(
            src_ref=src, dst_ref=dst, send_sem=send, recv_sem=recv,
            device_id={"lists": who}, device_id_type=pl.DeviceIdType.MESH,
        )

    def arrived(dst, sem):
        pltpu.make_async_copy(dst, dst, sem).wait()

    def send_meta(i):
        return remote(all_meta.at[me], all_meta.at[me], m_send.at[i], m_recv.at[me], other(i))

    def send_query(t):
        return remote(queries, all_q.at[me], q_send.at[t], q_recv.at[me], 2 * far(t) + side)

    def send_mate():
        return remote(queries, all_q.at[me], q_send.at[pairs_of - 1], q_recv.at[me], mate)

    def relay(t):
        who = 2 * far(pairs_of - 2 - t) + side
        return who, remote(all_q.at[who], all_q.at[who], q_send.at[pairs_of + t], q_recv.at[who], mate)

    def send_reply(l, i):
        who = other(i)
        return remote(reply.at[l, who], replies.at[l, me], r_send.at[l, i], r_recv.at[l, me], who)

    barrier = pltpu.get_barrier_semaphore()
    repeat(0, owners - 1, lambda i: pl.semaphore_signal(
        barrier, inc=1, device_id={"lists": other(i)}, device_id_type=pl.DeviceIdType.MESH))

    small = [pltpu.make_async_copy(list_slot, slot_of, slot_sem),
             pltpu.make_async_copy(probes, own_probes, probe_sem),
             pltpu.make_async_copy(cand, own_cand, cand_sem)]
    for copy in small:
        copy.start()
    pltpu.make_async_copy(queries, all_q.at[me], q_recv.at[me]).start()
    for l in range(local):
        pltpu.make_async_copy(corpus.at[l], lists.at[l], list_sem.at[l]).start()

    for copy in small:
        copy.wait()
    mine = own_probes[...]
    kinds = [mine] + [own_cand[:, c, :] for c in range(cand_count)]
    spare = jnp.zeros((probe_count, LANES - count * len(kinds)), jnp.int32)
    all_meta[me] = jnp.concatenate(kinds + [spare], axis=1)

    pl.semaphore_wait(barrier, owners - 1)
    send_mate().start()
    repeat(0, owners - 1, lambda i: send_meta(i).start())
    repeat(0, pairs_of - 1, lambda t: send_query(t).start())

    ids = iota((total, count), 0)
    named = jnp.zeros((total, count), f32)
    turn = jnp.zeros((total, count), f32)
    for p in range(probe_count):
        hit = ids == mine[p : p + 1, :]
        named = jnp.where(hit, 1.0, named)
        turn = jnp.where(hit, float(p), turn)
    turn = turn + named * (iota((total, count), 1) * probe_count + 1).astype(f32)
    held = iota((total, total), 0)
    to_slot = ((held % owners) * local + held // owners == slot_of[...]).astype(bf16)
    here = dot(to_slot, named.astype(bf16)).astype(bf16)
    turn = dot(to_slot, turn.astype(bf16))
    rank = dot(here, (iota((count, count), 0) < iota((count, count), 1)).astype(bf16))
    rank = lax.broadcast_in_dim(rank, (total, room, count), (0, 2))
    turn = lax.broadcast_in_dim(turn, (total, room, count), (0, 2))
    entry = jnp.where(rank == iota((total, room, count), 1).astype(f32), turn, 0.0)
    entry = entry.reshape(total * room, count).astype(bf16)
    target = dot(jnp.ones((8, count), bf16), entry, NT)[:1].astype(jnp.int32) - 1
    out_rows = iota((out.shape[0], total * room), 0)
    for c in range(cand_count):
        place[c] = (out_rows == target * cand_count + c).astype(bf16)

    step = min(length, 256)
    ones = jnp.ones((LANES, LANES), bf16)

    def thirds(x):
        high = x.astype(bf16)
        rest = x - high.astype(f32)
        mid = rest.astype(bf16)
        return high, mid, (rest - mid.astype(f32)).astype(bf16)

    def norms_of(l):
        pltpu.make_async_copy(corpus.at[l], lists.at[l], list_sem.at[l]).wait()

        def norms(k, carry):
            at = pl.multiple_of(k * step, step)
            part = jnp.zeros((step, LANES), f32)
            for j in range(0, features, LANES):
                x = lists[l, pl.ds(at, step), j : j + LANES].astype(f32)
                part = part + x * x
            high, mid, low = thirds(part)
            squares = dot(high, ones) + (dot(mid, ones) + dot(low, ones))
            inv_rows[l, pl.ds(at, step), :] = lax.rsqrt(squares / features + epsilon)
            return carry

        lax.fori_loop(0, length // step, norms, 0)

    def forward(t):
        who, copy = relay(t)
        arrived(all_q.at[who], q_recv.at[who])
        copy.start()

    norms_of(0)
    forward(0) if pairs_of > 1 else None
    for l in range(1, local):
        norms_of(l)
        if l < pairs_of - 1:
            forward(l)
    repeat(min(max(local, 1), pairs_of - 1), pairs_of - 1, forward)

    some = LANES // count
    rows = some * room
    lane = iota((rows, LANES), 1)
    row = iota((rows, LANES), 0)
    same = row // room == lane // count
    before = ((iota((LANES, LANES), 0) < iota((LANES, LANES), 1))
              & (iota((LANES, LANES), 0) // count == iota((LANES, LANES), 1) // count)).astype(bf16)

    def meta_here(i):
        arrived(all_meta.at[other(i)], m_recv.at[other(i)])

    repeat(0, owners - 1, meta_here)

    def index(k):
        asked, *blocks = [
            jnp.concatenate([all_meta[k * some + i, :, c * count : (c + 1) * count] for i in range(some)], axis=1)
            for c in range(1 + cand_count)]
        for l in range(local):
            name = jnp.sum(jnp.where(slot_of[...] == me * local + l, iota((1, total), 1), 0), axis=1, keepdims=True)
            hit = asked == name
            named = jnp.sum(jnp.where(hit, 1.0, 0.0), axis=0, keepdims=True)
            rank = dot(jnp.broadcast_to(named, (8, LANES)).astype(bf16), before)[:1]
            rank = jnp.where(named > 0.5, rank, -1.0)
            taken = same & (rank == (row % room).astype(f32))
            pick[l, pl.ds(k * rows, rows), :] = jnp.where(taken, 1.0, 0.0).astype(bf16)
            for c in range(cand_count):
                choice[l, k, c : c + 1, :] = jnp.sum(jnp.where(hit, blocks[c], 0), axis=0, keepdims=True)

    repeat(0, owners // some, index)

    arrived(all_q.at[me], q_recv.at[me])
    repeat(0, pairs_of, lambda t: arrived(all_q.at[2 * t + 1 - side], q_recv.at[2 * t + 1 - side]))

    scale = features ** (-0.5)

    def chunk_of(k):
        return all_q[pl.ds(k * some, some)].reshape(LANES, features)

    def query_norms(k):
        part = jnp.zeros((LANES, LANES), f32)
        for j in range(0, features, LANES):
            x = all_q[pl.ds(k * some, some), :, j : j + LANES].reshape(LANES, LANES).astype(f32)
            part = part + x * x
        high, mid, low = thirds(part)
        squares = dot(ones[:8], high, NT) + (dot(ones[:8], mid, NT) + dot(ones[:8], low, NT))
        inv_q[k] = lax.rsqrt(squares / features + epsilon)

    repeat(0, owners // some, query_norms)

    def score(l, carry):
        def of_chunk(k):
            products = dot(lists[l], chunk_of(k), NT)
            inverse = inv_q[k, :1, :]
            best = [None] * cand_count
            for b in range(length // BLOCK):
                at = slice(b * BLOCK, (b + 1) * BLOCK)
                block = products[at] * inverse * inv_rows[l, at, :] * scale
                for c in range(cand_count):
                    want = choice[l, k, c : c + 1, :] == b
                    best[c] = block if b == 0 else jnp.where(want, block, best[c])
            for c in range(cand_count):
                kept = dot(pick[l, pl.ds(k * rows, rows), :], best[c].astype(bf16), NT).astype(bf16)
                reply[l, pl.ds(k * some, some), :, c * BLOCK : (c + 1) * BLOCK] = kept.reshape(some, room, BLOCK)

        repeat(0, owners // some, of_chunk)
        repeat(0, owners - 1, lambda i: send_reply(l, i).start())
        pltpu.make_async_copy(reply.at[l, me], replies.at[l, me], r_recv.at[l, me]).start()
        return carry

    lax.fori_loop(0, local, score, 0)

    def answers(l, carry):
        repeat(0, owners, lambda o: arrived(replies.at[l, o], r_recv.at[l, o]))
        return carry

    lax.fori_loop(0, local, answers, 0)

    result = jnp.zeros(out.shape, f32)
    for c in range(cand_count):
        back = replies[:, :, :, c * LANES : (c + 1) * LANES].reshape(total * room, LANES)
        result = result + dot(place[c], back)
    out[...] = result.astype(bf16)

    send_mate().wait_send()
    repeat(0, pairs_of - 1, lambda t: send_query(t).wait_send())
    repeat(0, pairs_of - 1, lambda t: relay(t)[1].wait_send())
    repeat(0, owners - 1, lambda i: send_meta(i).wait_send())

    def sent(l, carry):
        repeat(0, owners - 1, lambda i: send_reply(l, i).wait_send())
        return carry

    lax.fori_loop(0, local, sent, 0)


def on_device(queries, corpus, list_slot, probes, cand):
    owners = lax.axis_size("lists")
    count, features = queries.shape
    probe_count = probes.shape[1]
    cand_count = cand.shape[2]
    local, length, _ = corpus.shape
    total = list_slot.shape[0]
    pairs = count * probe_count
    most = min(count, max(2, (2 * pairs + total - 1) // total))
    room = -(-most // 8) * 8
    vmem = pl.BlockSpec(memory_space=pltpu.VMEM)
    hbm = pl.BlockSpec(memory_space=pltpu.HBM)
    dma = pltpu.SemaphoreType.DMA
    wide = cand_count * LANES
    out = pl.pallas_call(
        functools.partial(kernel, owners),
        out_shape=jax.ShapeDtypeStruct((pairs * cand_count, BLOCK), bf16),
        in_specs=[hbm] * 5,
        out_specs=vmem,
        scratch_shapes=[
            pltpu.VMEM((owners, count, features), bf16),
            pltpu.VMEM(corpus.shape, bf16),
            pltpu.VMEM((1, total), jnp.int32),
            pltpu.VMEM((probe_count, count), jnp.int32),
            pltpu.VMEM((probe_count, cand_count, count), jnp.int32),
            pltpu.VMEM((owners, probe_count, LANES), jnp.int32),
            pltpu.VMEM((cand_count, pairs * cand_count, total * room), bf16),
            pltpu.VMEM((local, owners * room, LANES), bf16),
            pltpu.VMEM((local, owners * count // LANES, 8, LANES), jnp.int32),
            pltpu.VMEM((owners * count // LANES, 8, LANES), f32),
            pltpu.VMEM((local, length, LANES), f32),
            pltpu.VMEM((local, owners, room, wide), bf16),
            pltpu.VMEM((local, owners, room, wide), bf16),
            dma((owners,)), dma((owners,)), dma((owners,)), dma((owners,)),
            dma((local, owners)), dma((local, owners)), dma((local,)), dma, dma, dma,
        ],
        compiler_params=pltpu.CompilerParams(collective_id=0, has_side_effects=True, vmem_limit_bytes=48 * 2**20),
    )(*[pltpu.with_memory_space_constraint(x, pltpu.HBM) for x in (queries, corpus, list_slot.reshape(1, total), probes.T, cand.transpose(1, 2, 0))])
    return out.reshape(count, probe_count, cand_count, BLOCK)


def solution(mesh):
    placed = (
        P(("groups", "lists", "rep"), None),
        P(("groups", "lists"), None, None),
        P("groups"),
        P(("groups", "lists", "rep"), None),
        P(("groups", "lists", "rep"), None, None),
    )
    return jax.shard_map(
        on_device,
        mesh=mesh,
        in_specs=placed,
        out_specs=P(("groups", "lists", "rep"), None, None, None),
        check_vma=False,
    )
```

```python
import functools

import jax
import jax.numpy as jnp
from jax import lax
from jax.experimental import pallas as pl
from jax.experimental.pallas import tpu as pltpu
from jax.sharding import PartitionSpec as P

BLOCK = 128
LANES = 128
epsilon = 1e-06
f32, bf16 = jnp.float32, jnp.bfloat16
NN = (((1,), (0,)), ((), ()))
NT = (((1,), (1,)), ((), ()))


def dot(a, b, dims=NN):
    return lax.dot_general(a, b, dims, preferred_element_type=f32)


def iota(shape, axis):
    return lax.broadcasted_iota(jnp.int32, shape, axis)


def repeat(start, stop, body):
    if stop - start <= 8:
        for i in range(start, stop):
            body(i)
    else:
        lax.fori_loop(start, stop, lambda i, c: (body(i), c)[1], 0)


def kernel(
    owners, queries, corpus, list_slot, probes, cand, out,
    all_q, lists, slot_of, own_probes, own_cand, all_meta, place, pick, choice, inv_q, inv_rows, reply, replies,
    q_send, q_recv, m_send, m_recv, r_send, r_recv, list_sem, slot_sem, probe_sem, cand_sem,
):
    me = lax.axis_index("lists")
    local, length, features = lists.shape
    count = all_q.shape[1]
    total = list_slot.shape[1]
    probe_count = probes.shape[0]
    cand_count = cand.shape[1]
    room = replies.shape[2]
    pairs_of = owners // 2
    mate = me + 1 - 2 * (me % 2)
    side, spot = me % 2, me // 2

    def far(t):
        down = pairs_of - 1 - t
        down = down - jnp.where(down <= spot, 1, 0)
        up = t + jnp.where(t >= spot, 1, 0)
        return jnp.where(spot < pairs_of // 2, down, up)

    def other(i):
        if isinstance(i, int) and i == owners - 2:
            return mate
        there = 2 * far(i // 2) + i % 2
        return there if isinstance(i, int) else jnp.where(i == owners - 2, mate, there)

    def remote(src, dst, send, recv, who):
        return pltpu.make_async_remote_copy(
            src_ref=src, dst_ref=dst, send_sem=send, recv_sem=recv,
            device_id={"lists": who}, device_id_type=pl.DeviceIdType.MESH,
        )

    def arrived(dst, sem):
        pltpu.make_async_copy(dst, dst, sem).wait()

    def send_meta(i):
        return remote(all_meta.at[me], all_meta.at[me], m_send.at[i], m_recv.at[me], other(i))

    def send_query(t):
        return remote(queries, all_q.at[me], q_send.at[t], q_recv.at[me], 2 * far(t) + side)

    def send_mate():
        return remote(queries, all_q.at[me], q_send.at[pairs_of - 1], q_recv.at[me], mate)

    def relay(t):
        who = 2 * far(pairs_of - 2 - t) + side
        return who, remote(all_q.at[who], all_q.at[who], q_send.at[pairs_of + t], q_recv.at[who], mate)

    def send_reply(l, i):
        who = other(i)
        return remote(reply.at[l, who], replies.at[l, me], r_send.at[l, i], r_recv.at[l, me], who)

    barrier = pltpu.get_barrier_semaphore()
    repeat(0, owners - 1, lambda i: pl.semaphore_signal(
        barrier, inc=1, device_id={"lists": other(i)}, device_id_type=pl.DeviceIdType.MESH))

    small = [pltpu.make_async_copy(list_slot, slot_of, slot_sem),
             pltpu.make_async_copy(probes, own_probes, probe_sem),
             pltpu.make_async_copy(cand, own_cand, cand_sem)]
    for copy in small:
        copy.start()
    pltpu.make_async_copy(queries, all_q.at[me], q_recv.at[me]).start()
    for l in range(local):
        pltpu.make_async_copy(corpus.at[l], lists.at[l], list_sem.at[l]).start()

    pl.semaphore_wait(barrier, owners - 1)
    send_mate().start()
    repeat(0, pairs_of - 1, lambda t: send_query(t).start())

    for copy in small:
        copy.wait()
    mine = own_probes[...]
    kinds = [mine] + [own_cand[:, c, :] for c in range(cand_count)]
    spare = jnp.zeros((probe_count, LANES - count * len(kinds)), jnp.int32)
    all_meta[me] = jnp.concatenate(kinds + [spare], axis=1)
    repeat(0, owners - 1, lambda i: send_meta(i).start())

    ids = iota((total, count), 0)
    named = jnp.zeros((total, count), f32)
    turn = jnp.zeros((total, count), f32)
    for p in range(probe_count):
        hit = ids == mine[p : p + 1, :]
        named = jnp.where(hit, 1.0, named)
        turn = jnp.where(hit, float(p), turn)
    turn = turn + named * (iota((total, count), 1) * probe_count + 1).astype(f32)
    held = iota((total, total), 0)
    to_slot = ((held % owners) * local + held // owners == slot_of[...]).astype(bf16)
    here = dot(to_slot, named.astype(bf16)).astype(bf16)
    turn = dot(to_slot, turn.astype(bf16))
    rank = dot(here, (iota((count, count), 0) < iota((count, count), 1)).astype(bf16))
    rank = lax.broadcast_in_dim(rank, (total, room, count), (0, 2))
    turn = lax.broadcast_in_dim(turn, (total, room, count), (0, 2))
    entry = jnp.where(rank == iota((total, room, count), 1).astype(f32), turn, 0.0)
    entry = entry.reshape(total * room, count).astype(bf16)
    target = dot(jnp.ones((8, count), bf16), entry, NT)[:1].astype(jnp.int32) - 1
    out_rows = iota((out.shape[0], total * room), 0)
    for c in range(cand_count):
        place[c] = (out_rows == target * cand_count + c).astype(bf16)

    step = min(length, 256)
    ones = jnp.ones((LANES, LANES), bf16)

    def thirds(x):
        high = x.astype(bf16)
        rest = x - high.astype(f32)
        mid = rest.astype(bf16)
        return high, mid, (rest - mid.astype(f32)).astype(bf16)

    def norms_of(l):
        pltpu.make_async_copy(corpus.at[l], lists.at[l], list_sem.at[l]).wait()

        def norms(k, carry):
            at = pl.multiple_of(k * step, step)
            part = jnp.zeros((step, LANES), f32)
            for j in range(0, features, LANES):
                x = lists[l, pl.ds(at, step), j : j + LANES].astype(f32)
                part = part + x * x
            high, mid, low = thirds(part)
            squares = dot(high, ones) + (dot(mid, ones) + dot(low, ones))
            inv_rows[l, pl.ds(at, step), :] = lax.rsqrt(squares / features + epsilon)
            return carry

        lax.fori_loop(0, length // step, norms, 0)

    def forward(t):
        who, copy = relay(t)
        arrived(all_q.at[who], q_recv.at[who])
        copy.start()

    norms_of(0)
    forward(0) if pairs_of > 1 else None
    for l in range(1, local):
        norms_of(l)
        if l < pairs_of - 1:
            forward(l)
    repeat(min(max(local, 1), pairs_of - 1), pairs_of - 1, forward)

    some = LANES // count
    rows = some * room
    lane = iota((rows, LANES), 1)
    row = iota((rows, LANES), 0)
    same = row // room == lane // count
    before = ((iota((LANES, LANES), 0) < iota((LANES, LANES), 1))
              & (iota((LANES, LANES), 0) // count == iota((LANES, LANES), 1) // count)).astype(bf16)

    def meta_here(i):
        arrived(all_meta.at[other(i)], m_recv.at[other(i)])

    repeat(0, owners - 1, meta_here)

    def index(k):
        asked, *blocks = [
            jnp.concatenate([all_meta[k * some + i, :, c * count : (c + 1) * count] for i in range(some)], axis=1)
            for c in range(1 + cand_count)]
        for l in range(local):
            name = jnp.sum(jnp.where(slot_of[...] == me * local + l, iota((1, total), 1), 0), axis=1, keepdims=True)
            hit = asked == name
            named = jnp.sum(jnp.where(hit, 1.0, 0.0), axis=0, keepdims=True)
            rank = dot(jnp.broadcast_to(named, (8, LANES)).astype(bf16), before)[:1]
            rank = jnp.where(named > 0.5, rank, -1.0)
            taken = same & (rank == (row % room).astype(f32))
            pick[l, pl.ds(k * rows, rows), :] = jnp.where(taken, 1.0, 0.0).astype(bf16)
            for c in range(cand_count):
                choice[l, k, c : c + 1, :] = jnp.sum(jnp.where(hit, blocks[c], 0), axis=0, keepdims=True)

    repeat(0, owners // some, index)

    arrived(all_q.at[me], q_recv.at[me])
    repeat(0, pairs_of, lambda t: arrived(all_q.at[2 * t + 1 - side], q_recv.at[2 * t + 1 - side]))

    scale = features ** (-0.5)

    def chunk_of(k):
        return all_q[pl.ds(k * some, some)].reshape(LANES, features)

    def query_norms(k):
        part = jnp.zeros((LANES, LANES), f32)
        for j in range(0, features, LANES):
            x = all_q[pl.ds(k * some, some), :, j : j + LANES].reshape(LANES, LANES).astype(f32)
            part = part + x * x
        high, mid, low = thirds(part)
        squares = dot(ones[:8], high, NT) + (dot(ones[:8], mid, NT) + dot(ones[:8], low, NT))
        inv_q[k] = lax.rsqrt(squares / features + epsilon)

    repeat(0, owners // some, query_norms)

    def score(l, carry):
        def of_chunk(k):
            products = dot(lists[l], chunk_of(k), NT)
            inverse = inv_q[k, :1, :]
            best = [None] * cand_count
            for b in range(length // BLOCK):
                at = slice(b * BLOCK, (b + 1) * BLOCK)
                block = products[at] * inverse * inv_rows[l, at, :] * scale
                for c in range(cand_count):
                    want = choice[l, k, c : c + 1, :] == b
                    best[c] = block if b == 0 else jnp.where(want, block, best[c])
            for c in range(cand_count):
                kept = dot(pick[l, pl.ds(k * rows, rows), :], best[c].astype(bf16), NT).astype(bf16)
                reply[l, pl.ds(k * some, some), :, c * BLOCK : (c + 1) * BLOCK] = kept.reshape(some, room, BLOCK)

        repeat(0, owners // some, of_chunk)
        repeat(0, owners - 1, lambda i: send_reply(l, i).start())
        pltpu.make_async_copy(reply.at[l, me], replies.at[l, me], r_recv.at[l, me]).start()
        return carry

    lax.fori_loop(0, local, score, 0)

    def answers(l, carry):
        repeat(0, owners, lambda o: arrived(replies.at[l, o], r_recv.at[l, o]))
        return carry

    lax.fori_loop(0, local, answers, 0)

    result = jnp.zeros(out.shape, f32)
    for c in range(cand_count):
        back = replies[:, :, :, c * LANES : (c + 1) * LANES].reshape(total * room, LANES)
        result = result + dot(place[c], back)
    out[...] = result.astype(bf16)

    send_mate().wait_send()
    repeat(0, pairs_of - 1, lambda t: send_query(t).wait_send())
    repeat(0, pairs_of - 1, lambda t: relay(t)[1].wait_send())
    repeat(0, owners - 1, lambda i: send_meta(i).wait_send())

    def sent(l, carry):
        repeat(0, owners - 1, lambda i: send_reply(l, i).wait_send())
        return carry

    lax.fori_loop(0, local, sent, 0)


def on_device(queries, corpus, list_slot, probes, cand):
    owners = lax.axis_size("lists")
    count, features = queries.shape
    probe_count = probes.shape[1]
    cand_count = cand.shape[2]
    local, length, _ = corpus.shape
    total = list_slot.shape[0]
    pairs = count * probe_count
    most = min(count, max(2, (2 * pairs + total - 1) // total))
    room = -(-most // 8) * 8
    vmem = pl.BlockSpec(memory_space=pltpu.VMEM)
    hbm = pl.BlockSpec(memory_space=pltpu.HBM)
    dma = pltpu.SemaphoreType.DMA
    wide = cand_count * LANES
    out = pl.pallas_call(
        functools.partial(kernel, owners),
        out_shape=jax.ShapeDtypeStruct((pairs * cand_count, BLOCK), bf16),
        in_specs=[hbm] * 5,
        out_specs=vmem,
        scratch_shapes=[
            pltpu.VMEM((owners, count, features), bf16),
            pltpu.VMEM(corpus.shape, bf16),
            pltpu.VMEM((1, total), jnp.int32),
            pltpu.VMEM((probe_count, count), jnp.int32),
            pltpu.VMEM((probe_count, cand_count, count), jnp.int32),
            pltpu.VMEM((owners, probe_count, LANES), jnp.int32),
            pltpu.VMEM((cand_count, pairs * cand_count, total * room), bf16),
            pltpu.VMEM((local, owners * room, LANES), bf16),
            pltpu.VMEM((local, owners * count // LANES, 8, LANES), jnp.int32),
            pltpu.VMEM((owners * count // LANES, 8, LANES), f32),
            pltpu.VMEM((local, length, LANES), f32),
            pltpu.VMEM((local, owners, room, wide), bf16),
            pltpu.VMEM((local, owners, room, wide), bf16),
            dma((owners,)), dma((owners,)), dma((owners,)), dma((owners,)),
            dma((local, owners)), dma((local, owners)), dma((local,)), dma, dma, dma,
        ],
        compiler_params=pltpu.CompilerParams(collective_id=0, has_side_effects=True, vmem_limit_bytes=48 * 2**20),
    )(*[pltpu.with_memory_space_constraint(x, pltpu.HBM) for x in (queries, corpus, list_slot.reshape(1, total), probes.T, cand.transpose(1, 2, 0))])
    return out.reshape(count, probe_count, cand_count, BLOCK)


def solution(mesh):
    placed = (
        P(("groups", "lists", "rep"), None),
        P(("groups", "lists"), None, None),
        P("groups"),
        P(("groups", "lists", "rep"), None),
        P(("groups", "lists", "rep"), None, None),
    )
    return jax.shard_map(
        on_device,
        mesh=mesh,
        in_specs=placed,
        out_specs=P(("groups", "lists", "rep"), None, None, None),
        check_vma=False,
    )
```

```python
import functools

import jax
import jax.numpy as jnp
from jax import lax
from jax.experimental import pallas as pl
from jax.experimental.pallas import tpu as pltpu
from jax.sharding import PartitionSpec as P

BLOCK = 128
LANES = 128
epsilon = 1e-06
f32, bf16 = jnp.float32, jnp.bfloat16
NN = (((1,), (0,)), ((), ()))
NT = (((1,), (1,)), ((), ()))


def dot(a, b, dims=NN):
    return lax.dot_general(a, b, dims, preferred_element_type=f32)


def iota(shape, axis):
    return lax.broadcasted_iota(jnp.int32, shape, axis)


def repeat(start, stop, body):
    if stop - start <= 8:
        for i in range(start, stop):
            body(i)
    else:
        lax.fori_loop(start, stop, lambda i, c: (body(i), c)[1], 0)


def kernel(
    owners, queries, corpus, list_slot, probes, cand, out,
    all_q, lists, slot_of, own_probes, own_cand, all_meta, place, pick, choice, inv_q, inv_rows, reply, replies,
    q_send, q_recv, m_send, m_recv, r_send, r_recv, list_sem, slot_sem, probe_sem, cand_sem,
):
    me = lax.axis_index("lists")
    local, length, features = lists.shape
    count = all_q.shape[1]
    total = list_slot.shape[1]
    probe_count = probes.shape[0]
    cand_count = cand.shape[1]
    room = replies.shape[2]
    pairs_of = owners // 2
    mate = me + 1 - 2 * (me % 2)
    side, spot = me % 2, me // 2

    def far(t):
        down = pairs_of - 1 - t
        down = down - jnp.where(down <= spot, 1, 0)
        up = t + jnp.where(t >= spot, 1, 0)
        return jnp.where(spot < pairs_of // 2, down, up)

    def other(i):
        if isinstance(i, int) and i == owners - 2:
            return mate
        there = 2 * far(i // 2) + i % 2
        return there if isinstance(i, int) else jnp.where(i == owners - 2, mate, there)

    def remote(src, dst, send, recv, who):
        return pltpu.make_async_remote_copy(
            src_ref=src, dst_ref=dst, send_sem=send, recv_sem=recv,
            device_id={"lists": who}, device_id_type=pl.DeviceIdType.MESH,
        )

    def arrived(dst, sem):
        pltpu.make_async_copy(dst, dst, sem).wait()

    def send_meta(t):
        who = mate if isinstance(t, int) and t == pairs_of - 1 else 2 * far(t) + side
        return remote(all_meta.at[me], all_meta.at[me], m_send.at[t], m_recv.at[me], who)

    def relay_meta(t):
        who = 2 * far(pairs_of - 2 - t) + side
        return remote(all_meta.at[who], all_meta.at[who], m_send.at[pairs_of + t], m_recv.at[who], mate)

    def send_query(t):
        return remote(queries, all_q.at[me], q_send.at[t], q_recv.at[me], 2 * far(t) + side)

    def send_mate():
        return remote(queries, all_q.at[me], q_send.at[pairs_of - 1], q_recv.at[me], mate)

    def relay(t):
        who = 2 * far(pairs_of - 2 - t) + side
        return who, remote(all_q.at[who], all_q.at[who], q_send.at[pairs_of + t], q_recv.at[who], mate)

    def send_reply(l, i):
        who = other(i)
        return remote(reply.at[l, who], replies.at[l, me], r_send.at[l, i], r_recv.at[l, me], who)

    barrier = pltpu.get_barrier_semaphore()
    repeat(0, pairs_of - 1, lambda i: pl.semaphore_signal(
        barrier, inc=1, device_id={"lists": 2*far(i)+side}, device_id_type=pl.DeviceIdType.MESH))
    pl.semaphore_signal(barrier, inc=1, device_id={"lists": mate}, device_id_type=pl.DeviceIdType.MESH)

    small = [pltpu.make_async_copy(list_slot, slot_of, slot_sem),
             pltpu.make_async_copy(probes, own_probes, probe_sem),
             pltpu.make_async_copy(cand, own_cand, cand_sem)]
    for copy in small:
        copy.start()
    pltpu.make_async_copy(queries, all_q.at[me], q_recv.at[me]).start()
    for l in range(local):
        pltpu.make_async_copy(corpus.at[l], lists.at[l], list_sem.at[l]).start()

    pl.semaphore_wait(barrier, pairs_of)
    send_mate().start()
    repeat(0, pairs_of - 1, lambda t: send_query(t).start())

    for copy in small:
        copy.wait()
    mine = own_probes[...]
    kinds = [mine] + [own_cand[:, c, :] for c in range(cand_count)]
    spare = jnp.zeros((probe_count, LANES - count * len(kinds)), jnp.int32)
    all_meta[me] = jnp.concatenate(kinds + [spare], axis=1)
    send_meta(pairs_of - 1).start()
    repeat(0, pairs_of - 1, lambda t: send_meta(t).start())

    step = min(length, 256)
    ones = jnp.ones((LANES, LANES), bf16)

    def thirds(x):
        high = x.astype(bf16)
        rest = x - high.astype(f32)
        mid = rest.astype(bf16)
        return high, mid, (rest - mid.astype(f32)).astype(bf16)

    def norms_of(l):
        pltpu.make_async_copy(corpus.at[l], lists.at[l], list_sem.at[l]).wait()

        def norms(k, carry):
            at = pl.multiple_of(k * step, step)
            part = jnp.zeros((step, LANES), f32)
            for j in range(0, features, LANES):
                x = lists[l, pl.ds(at, step), j : j + LANES].astype(f32)
                part = part + x * x
            high, mid, low = thirds(part)
            squares = dot(high, ones) + (dot(mid, ones) + dot(low, ones))
            inv_rows[l, pl.ds(at, step), :] = lax.rsqrt(squares / features + epsilon)
            return carry

        lax.fori_loop(0, length // step, norms, 0)

    def forward(t):
        who, copy = relay(t)
        arrived(all_q.at[who], q_recv.at[who])
        copy.start()
        arrived(all_meta.at[who], m_recv.at[who])
        relay_meta(t).start()

    norms_of(0)
    forward(0) if pairs_of > 1 else None
    for l in range(1, local):
        norms_of(l)
        if l < pairs_of - 1:
            forward(l)
    repeat(min(max(local, 1), pairs_of - 1), pairs_of - 1, forward)

    ids = iota((total, count), 0)
    named = jnp.zeros((total, count), f32)
    turn = jnp.zeros((total, count), f32)
    for p in range(probe_count):
        hit = ids == mine[p : p + 1, :]
        named = jnp.where(hit, 1.0, named)
        turn = jnp.where(hit, float(p), turn)
    turn = turn + named * (iota((total, count), 1) * probe_count + 1).astype(f32)
    held = iota((total, total), 0)
    to_slot = ((held % owners) * local + held // owners == slot_of[...]).astype(bf16)
    here = dot(to_slot, named.astype(bf16)).astype(bf16)
    turn = dot(to_slot, turn.astype(bf16))
    rank = dot(here, (iota((count, count), 0) < iota((count, count), 1)).astype(bf16))
    rank = lax.broadcast_in_dim(rank, (total, room, count), (0, 2))
    turn = lax.broadcast_in_dim(turn, (total, room, count), (0, 2))
    entry = jnp.where(rank == iota((total, room, count), 1).astype(f32), turn, 0.0)
    entry = entry.reshape(total * room, count).astype(bf16)
    target = dot(jnp.ones((8, count), bf16), entry, NT)[:1].astype(jnp.int32) - 1
    out_rows = iota((out.shape[0], total * room), 0)
    for c in range(cand_count):
        place[c] = (out_rows == target * cand_count + c).astype(bf16)

    some = LANES // count
    rows = some * room
    lane = iota((rows, LANES), 1)
    row = iota((rows, LANES), 0)
    same = row // room == lane // count
    before = ((iota((LANES, LANES), 0) < iota((LANES, LANES), 1))
              & (iota((LANES, LANES), 0) // count == iota((LANES, LANES), 1) // count)).astype(bf16)

    repeat(0, pairs_of, lambda t: arrived(all_meta.at[2 * t + 1 - side], m_recv.at[2 * t + 1 - side]))

    def index(k):
        asked, *blocks = [
            jnp.concatenate([all_meta[k * some + i, :, c * count : (c + 1) * count] for i in range(some)], axis=1)
            for c in range(1 + cand_count)]
        for l in range(local):
            name = jnp.sum(jnp.where(slot_of[...] == me * local + l, iota((1, total), 1), 0), axis=1, keepdims=True)
            hit = asked == name
            named = jnp.sum(jnp.where(hit, 1.0, 0.0), axis=0, keepdims=True)
            rank = dot(jnp.broadcast_to(named, (8, LANES)).astype(bf16), before)[:1]
            rank = jnp.where(named > 0.5, rank, -1.0)
            taken = same & (rank == (row % room).astype(f32))
            pick[l, pl.ds(k * rows, rows), :] = jnp.where(taken, 1.0, 0.0).astype(bf16)
            for c in range(cand_count):
                choice[l, k, c : c + 1, :] = jnp.sum(jnp.where(hit, blocks[c], 0), axis=0, keepdims=True)

    repeat(0, owners // some, index)

    arrived(all_q.at[me], q_recv.at[me])
    repeat(0, pairs_of, lambda t: arrived(all_q.at[2 * t + 1 - side], q_recv.at[2 * t + 1 - side]))

    scale = features ** (-0.5)

    def chunk_of(k):
        return all_q[pl.ds(k * some, some)].reshape(LANES, features)

    def query_norms(k):
        part = jnp.zeros((LANES, LANES), f32)
        for j in range(0, features, LANES):
            x = all_q[pl.ds(k * some, some), :, j : j + LANES].reshape(LANES, LANES).astype(f32)
            part = part + x * x
        high, mid, low = thirds(part)
        squares = dot(ones[:8], high, NT) + (dot(ones[:8], mid, NT) + dot(ones[:8], low, NT))
        inv_q[k] = lax.rsqrt(squares / features + epsilon)

    repeat(0, owners // some, query_norms)

    def score(l, carry):
        def of_chunk(k):
            products = dot(lists[l], chunk_of(k), NT)
            inverse = inv_q[k, :1, :]
            best = [None] * cand_count
            for b in range(length // BLOCK):
                at = slice(b * BLOCK, (b + 1) * BLOCK)
                block = products[at] * inverse * inv_rows[l, at, :] * scale
                for c in range(cand_count):
                    want = choice[l, k, c : c + 1, :] == b
                    best[c] = block if b == 0 else jnp.where(want, block, best[c])
            for c in range(cand_count):
                kept = dot(pick[l, pl.ds(k * rows, rows), :], best[c].astype(bf16), NT).astype(bf16)
                reply[l, pl.ds(k * some, some), :, c * BLOCK : (c + 1) * BLOCK] = kept.reshape(some, room, BLOCK)

        repeat(0, owners // some, of_chunk)
        repeat(0, owners - 1, lambda i: send_reply(l, i).start())
        pltpu.make_async_copy(reply.at[l, me], replies.at[l, me], r_recv.at[l, me]).start()
        return carry

    lax.fori_loop(0, local, score, 0)

    def answers(l, carry):
        repeat(0, owners, lambda o: arrived(replies.at[l, o], r_recv.at[l, o]))
        return carry

    lax.fori_loop(0, local, answers, 0)

    result = jnp.zeros(out.shape, f32)
    for c in range(cand_count):
        back = replies[:, :, :, c * LANES : (c + 1) * LANES].reshape(total * room, LANES)
        result = result + dot(place[c], back)
    out[...] = result.astype(bf16)

    send_mate().wait_send()
    repeat(0, pairs_of - 1, lambda t: send_query(t).wait_send())
    repeat(0, pairs_of - 1, lambda t: relay(t)[1].wait_send())
    send_meta(pairs_of - 1).wait_send()
    repeat(0, pairs_of - 1, lambda t: send_meta(t).wait_send())
    repeat(0, pairs_of - 1, lambda t: relay_meta(t).wait_send())

    def sent(l, carry):
        repeat(0, owners - 1, lambda i: send_reply(l, i).wait_send())
        return carry

    lax.fori_loop(0, local, sent, 0)


def on_device(queries, corpus, list_slot, probes, cand):
    owners = lax.axis_size("lists")
    count, features = queries.shape
    probe_count = probes.shape[1]
    cand_count = cand.shape[2]
    local, length, _ = corpus.shape
    total = list_slot.shape[0]
    pairs = count * probe_count
    most = min(count, max(2, (2 * pairs + total - 1) // total))
    room = -(-most // 8) * 8
    vmem = pl.BlockSpec(memory_space=pltpu.VMEM)
    hbm = pl.BlockSpec(memory_space=pltpu.HBM)
    dma = pltpu.SemaphoreType.DMA
    wide = cand_count * LANES
    out = pl.pallas_call(
        functools.partial(kernel, owners),
        out_shape=jax.ShapeDtypeStruct((pairs * cand_count, BLOCK), bf16),
        in_specs=[hbm] * 5,
        out_specs=vmem,
        scratch_shapes=[
            pltpu.VMEM((owners, count, features), bf16),
            pltpu.VMEM(corpus.shape, bf16),
            pltpu.VMEM((1, total), jnp.int32),
            pltpu.VMEM((probe_count, count), jnp.int32),
            pltpu.VMEM((probe_count, cand_count, count), jnp.int32),
            pltpu.VMEM((owners, probe_count, LANES), jnp.int32),
            pltpu.VMEM((cand_count, pairs * cand_count, total * room), bf16),
            pltpu.VMEM((local, owners * room, LANES), bf16),
            pltpu.VMEM((local, owners * count // LANES, 8, LANES), jnp.int32),
            pltpu.VMEM((owners * count // LANES, 8, LANES), f32),
            pltpu.VMEM((local, length, LANES), f32),
            pltpu.VMEM((local, owners, room, wide), bf16),
            pltpu.VMEM((local, owners, room, wide), bf16),
            dma((owners,)), dma((owners,)), dma((owners,)), dma((owners,)),
            dma((local, owners)), dma((local, owners)), dma((local,)), dma, dma, dma,
        ],
        compiler_params=pltpu.CompilerParams(collective_id=0, has_side_effects=True, vmem_limit_bytes=48 * 2**20),
    )(*[pltpu.with_memory_space_constraint(x, pltpu.HBM) for x in (queries, corpus, list_slot.reshape(1, total), probes.T, cand.transpose(1, 2, 0))])
    return out.reshape(count, probe_count, cand_count, BLOCK)


def solution(mesh):
    placed = (
        P(("groups", "lists", "rep"), None),
        P(("groups", "lists"), None, None),
        P("groups"),
        P(("groups", "lists", "rep"), None),
        P(("groups", "lists", "rep"), None, None),
    )
    return jax.shard_map(
        on_device,
        mesh=mesh,
        in_specs=placed,
        out_specs=P(("groups", "lists", "rep"), None, None, None),
        check_vma=False,
    )
```
